512 devices in a mesh: gx: 16 (over z, core), gy: 32 (over x, y).
Axes of the slice: x: 4, y: 8, z: 8, core: 2. Of those that a mesh axis runs over, the one named last changes fastest.
Arguments:
- right_side: float32 [2, 2048, 4096], P(None, 'gx', 'gy'), may hold values from -6 to 6
- shift_coef: float32 [2048, 4096], P('gx', 'gy'), may hold values from 0.0001 to 0.001
- viscosity: float32 [2048, 4096], P('gx', 'gy'), may hold values from 1 to 10
- wet_tiles: int32 [16, 32], P('gx', 'gy'), may hold values from 0 to 1, as said below
Outputs:
- velocity: float32 [2, 2048, 4096], P(None, 'gx', 'gy')
The draws below stay inside these ranges and needn't reach their ends.
Inputs may be any that keep to these rules, and one draw needn't show every extreme that they name: `wet_tiles`: 1 marks a wet tile of 128 x 128 cells, 0 a dry one.
All inputs are finite; a program needn't handle non-finite values.
Results may differ from the reference program's by a relative error of at most 0.00002.
Values sent between devices are 32-bit elements; how exact they have to be, the bound alone decides.
A program may use at most 64 MiB of HBM per device.

```python
import math
import jax
import jax.numpy as jnp
from jax import lax

TILE = 128
LOCAL = 4
COARSE = 4
COARSE_SWEEPS = 8
NX = 2048
NY = 4096


def draw_wet_tiles(key, part):
    tile_rows = NX // TILE
    tile_cols = NY // TILE
    position = lax.broadcasted_iota(jnp.int32, (tile_rows, tile_cols), 0)
    threshold = 40 + 55 * position // max(tile_rows - 1, 1)
    rolled = jax.random.randint(key, (tile_rows, tile_cols), 0, 100)
    return (rolled < threshold).astype(jnp.int32)


def levels(stream_key, dims, pieces, low, top_value):
    def one(dim, parts):
        draws = jax.random.uniform(jax.random.fold_in(jax.random.fold_in(stream_key, 6), dim), (parts,), jnp.float32, low / len(pieces), top_value / len(pieces))
        return jnp.repeat(jnp.exp(draws), dims[dim] // parts).reshape((-1,) + (1,) * (len(dims) - dim - 1))

    factor_of = one(*pieces[0])
    for cut in pieces[1:]:
        factor_of = factor_of * one(*cut)
    return factor_of


def bell_draw(stream_key, extent, scale, most, shards=(), kind=jnp.bfloat16):
    values = scale * jax.random.normal(stream_key, extent, jnp.float32)
    if shards:
        values = values * levels(stream_key, extent, shards, -0.22, 0.18)
    return jnp.clip(values, -most, most).astype(kind)


def setup_inputs(seed: int = 0) -> dict:
    splits = jax.random.split(jax.random.key(seed), 5)
    right_side = bell_draw(splits[0], (2, NX, NY), 1.0, 6.0, ((1, 16), (2, 32)), jnp.float32)
    shift_coef = jnp.clip(jnp.exp(math.log(0.001) - 2.3025852 * jax.random.uniform(splits[1], (NX, NY), jnp.float32) ** levels(splits[1], (NX, NY), ((0, 16), (1, 32)), -0.2, 0.2)), 0.0001, 0.001)
    viscosity = jnp.clip(jnp.exp(math.log(10.0) - 2.3025851 * jax.random.uniform(splits[2], (NX, NY), jnp.float32) ** levels(splits[2], (NX, NY), ((0, 16), (1, 32)), -0.2, 0.2)), 1.0, 10.0)
    wet_tiles = draw_wet_tiles(jax.random.fold_in(splits[4], 71), 0)
    return {"right_side": right_side, "shift_coef": shift_coef, "viscosity": viscosity, "wet_tiles": wet_tiles}


OMEGA = 0.8


def pad_last(field):
    return jnp.pad(field, [(0, 0)] * (field.ndim - 2) + [(1, 1), (1, 1)])


def face_coefs(padded):
    inner = padded[1:-1, 1:-1]
    return jnp.stack([jnp.minimum(inner, padded[:-2, 1:-1]), jnp.minimum(inner, padded[2:, 1:-1]),
                      jnp.minimum(inner, padded[1:-1, :-2]), jnp.minimum(inner, padded[1:-1, 2:])])


def apply_padded(padded, conduct, reaction, spacing):
    inner = padded[:, 1:-1, 1:-1]
    outflow = conduct[0] * (inner - padded[:, :-2, 1:-1]) + conduct[1] * (inner - padded[:, 2:, 1:-1])
    outflow = outflow + conduct[2] * (inner - padded[:, 1:-1, :-2]) + conduct[3] * (inner - padded[:, 1:-1, 2:])
    return reaction * inner + spacing * outflow


def shrink(field):
    size_x, size_y = field.shape[-2:]
    blocks = field.reshape(field.shape[:-2] + (size_x // 2, 2, size_y // 2, 2))
    return jnp.mean(blocks, axis=(-3, -1))


def widen(field):
    return jnp.repeat(jnp.repeat(field, 2, axis=-2), 2, axis=-1)


def level_solve(grid_level, source, reaction, viscous):
    conduct = face_coefs(pad_last(viscous))
    spacing = 0.25 ** grid_level
    diagonal = reaction + spacing * jnp.sum(conduct, axis=0)
    if grid_level == LOCAL + COARSE:
        iterate = jnp.zeros_like(source)
        for sweep_index in range(COARSE_SWEEPS):
            iterate = iterate + OMEGA * (source - apply_padded(pad_last(iterate), conduct, reaction, spacing)) / diagonal
        return iterate
    iterate = OMEGA * source / diagonal
    residual = source - apply_padded(pad_last(iterate), conduct, reaction, spacing)
    correction = level_solve(grid_level + 1, shrink(residual), shrink(reaction), shrink(viscous))
    iterate = iterate + widen(correction)
    return iterate + OMEGA * (source - apply_padded(pad_last(iterate), conduct, reaction, spacing)) / diagonal


def reference(right_side, shift_coef, viscosity, wet_tiles):
    wetness = jnp.repeat(jnp.repeat(wet_tiles, TILE, axis=0), TILE, axis=1).astype(jnp.float32)
    return level_solve(0, right_side * wetness, shift_coef, viscosity * wetness)
```

```python
import functools

import jax
import jax.numpy as jnp
from jax import lax
from jax.experimental import pallas as pl
from jax.experimental.pallas import tpu as pltpu
from jax.sharding import PartitionSpec as P

TILE = 128
OMEGA = 0.8
KEEP = 1.0 - OMEGA
HALO = 16
ROWS = TILE + 2 * HALO
F32 = jnp.float32
MESH = pl.DeviceIdType.MESH
DIRECTIONS = ((-1, 0), (1, 0), (0, -1), (0, 1), (-1, -1), (-1, 1), (1, -1), (1, 1))
SOURCE_OF = {step: i for i, step in enumerate(DIRECTIONS)}


def iota(shape, dim):
    return lax.broadcasted_iota(jnp.int32, shape, dim)


def roll_rows(x, k):
    return pltpu.roll(x, k % x.shape[0], axis=0)


def roll_lanes(x, k):
    return pltpu.roll(x, k % x.shape[1], axis=1)


def exact_dot(a, b, transposed=False):
    dims = (((1,), (1,)), ((), ())) if transposed else (((1,), (0,)), ((), ()))
    return lax.dot_general(
        a, b, dims, precision=lax.Precision.HIGHEST, preferred_element_type=F32
    )


def coefficients(viscous, reaction, level, pitch, closed=None):
    spacing = 0.25**level
    up = jnp.minimum(viscous, roll_rows(viscous, 1)) * spacing
    left = jnp.minimum(viscous, roll_lanes(viscous, pitch)) * spacing
    if closed is not None:
        up = jnp.where(closed[0], 0.0, up)
        left = jnp.where(closed[1], 0.0, left)
    down = roll_rows(up, -1)
    right = roll_lanes(left, -pitch)
    weight = OMEGA / (reaction + ((up + down) + (left + right)))
    return up, down, left, right, weight


def inflow(iterate, faces, pitch):
    up, down, left, right = faces[:4]
    return (up * roll_rows(iterate, 1) + down * roll_rows(iterate, -1)) + (
        left * roll_lanes(iterate, pitch) + right * roll_lanes(iterate, -pitch)
    )


def residual_of(source, iterate, faces, pitch):
    return KEEP * source + inflow(iterate, faces, pitch)


def swept(source, iterate, faces, pitch):
    return KEEP * iterate + faces[4] * (source + inflow(iterate, faces, pitch))


def kernel(
    gx_count,
    gy_count,
    rhs_hbm,
    shift_hbm,
    visc_hbm,
    wet_ref,
    out_ref,
    own,
    strips,
    coef_block,
    row_halo,
    col_halo,
    corner_halo,
    coef_halo,
    block,
    block_halo,
    gx_coef,
    gx_source,
    gy_coef,
    gy_source,
    ext,
    pooled,
    level0,
    level1,
    level2,
    padded,
    spread,
    coarse,
    load_sem,
    send1,
    recv1,
    send2,
    recv2,
    send3,
    recv3,
    gather_send,
    gather_recv,
):
    a = lax.axis_index("gx")
    b = lax.axis_index("gy")

    def at(da, db):
        return (lax.rem(a + da + gx_count, gx_count), lax.rem(b + db + gy_count, gy_count))

    barrier = pltpu.get_barrier_semaphore()

    def greet_gx(k, carry):
        peer = (lax.rem(a + k, gx_count), b)
        pl.semaphore_signal(barrier, inc=1, device_id=peer, device_id_type=MESH)
        return carry

    def greet_gy(k, carry):
        peer = (a, lax.rem(b + k, gy_count))
        pl.semaphore_signal(barrier, inc=1, device_id=peer, device_id_type=MESH)
        return carry

    for da, db in DIRECTIONS[4:]:
        pl.semaphore_signal(barrier, inc=1, device_id=at(da, db), device_id_type=MESH)
    lax.fori_loop(1, gx_count, greet_gx, 0)
    lax.fori_loop(1, gy_count, greet_gy, 0)

    loads = [
        pltpu.make_async_copy(rhs_hbm, own.at[pl.ds(0, 2)], load_sem.at[0]),
        pltpu.make_async_copy(shift_hbm, own.at[2], load_sem.at[1]),
        pltpu.make_async_copy(visc_hbm, own.at[3], load_sem.at[2]),
    ]
    for load in loads:
        load.start()

    padded[...] = jnp.zeros_like(padded)
    for load in loads:
        load.wait()

    wet = wet_ref[0, 0].astype(F32)
    for f in (0, 1, 3):
        own[f] = own[f] * wet

    slot = iota((64, 128), 1) // HALO
    for side, first in ((0, 0), (1, TILE - HALO)):
        packed = jnp.zeros((64, 128), F32)
        for half in range(2):
            for f in range(4):
                place = half * 64 + f * HALO
                moved = roll_lanes(own[f, half * 64 : half * 64 + 64, :], place - first)
                packed = jnp.where(slot == half * 4 + f, moved, packed)
        strips[side] = packed

    lane_to_col = jnp.where(iota((16, 128), 1) // 8 == iota((16, 128), 0), 0.125, 0.0)
    target = iota((128, 128), 1)
    target_row = jnp.where(target < 48, target, jnp.where(target < 96, target - 48, -1)) - 16
    row_to_lane = jnp.where(iota((128, 128), 0) // 8 == target_row, 0.125, 0.0)
    for i, f in enumerate((2, 3)):
        coef_block[i] = exact_dot(exact_dot(lane_to_col, own[f], True), row_to_lane)

    pl.semaphore_wait(barrier, 4 + gx_count - 1 + gy_count - 1)

    copies1 = []

    def send(src, dst, sends, recvs, i, da, db):
        copy = pltpu.make_async_remote_copy(
            src_ref=src,
            dst_ref=dst,
            send_sem=sends.at[i],
            recv_sem=recvs.at[i],
            device_id=at(da, db),
            device_id_type=MESH,
        )
        copy.start()
        return copy

    for i, (da, db) in enumerate(DIRECTIONS):
        if db == 0:
            first = 0 if da < 0 else TILE - HALO
            src, dst = own.at[:, pl.ds(first, HALO)], row_halo.at[i]
        elif da == 0:
            src, dst = strips.at[0 if db < 0 else 1], col_halo.at[i - 2]
        else:
            first = 0 if da < 0 else 64 - HALO
            src = strips.at[0 if db < 0 else 1, pl.ds(first, HALO)]
            dst = corner_halo.at[i - 4]
        copies1.append(send(src, dst, send1, recv1, i, da, db))
    copies2 = [
        send(coef_block, coef_halo.at[i], send2, recv2, i, da, db)
        for i, (da, db) in enumerate(DIRECTIONS)
    ]

    lane = iota((1, 128), 1)
    inside_up = (a > 0).astype(F32)
    inside_down = (a < gx_count - 1).astype(F32)
    inside_left = (b > 0).astype(F32)
    inside_right = (b < gy_count - 1).astype(F32)
    for f in range(4):
        ext[f, HALO : HALO + TILE, 0:128] = own[f]

    for copy in copies1:
        copy.wait()

    from_down, from_up = row_halo[0], row_halo[1]
    visible = (lane < HALO).astype(F32) * inside_right + (lane >= TILE - HALO).astype(
        F32
    ) * inside_left
    for f in range(4):
        top, bottom = from_up[f], from_down[f]
        if f == 3:
            top, bottom = top * inside_up, bottom * inside_down
        ext[f, 0:HALO, 0:128] = top
        ext[f, HALO + TILE :, 0:128] = bottom
        fill = 1.0 if f == 2 else 0.0

        def side(right, left, half):
            place = half * 64 + f * HALO
            r = roll_lanes(right, -place)
            l = roll_lanes(left, TILE - HALO - place)
            both = jnp.where(lane < HALO, r, jnp.where(lane >= TILE - HALO, l, fill))
            return both * visible if f == 3 else both

        for half in range(2):
            ext[f, HALO + half * 64 : HALO + half * 64 + 64, 128:256] = side(
                col_halo[0], col_halo[1], half
            )
        top = side(corner_halo[2], corner_halo[3], 1)
        bottom = side(corner_halo[0], corner_halo[1], 0)
        if f == 3:
            top, bottom = top * inside_up, bottom * inside_down
        ext[f, 0:HALO, 128:256] = top
        ext[f, HALO + TILE :, 128:256] = bottom

    def pool(x, i, pitch, start=0, rows=None):
        n = x.shape[0]
        width = x.shape[1]
        rows = n // 2 if rows is None else rows
        parts = []
        for t in range(width // 128):
            pooled[i, t, 0:n, :] = x[:, t * 128 : t * 128 + 128]
            parts.append(
                pooled[i, t, pl.ds(start, rows, stride=2), :]
                + pooled[i, t, pl.ds(start + 1, rows, stride=2), :]
            )
        y = parts[0] if len(parts) == 1 else jnp.concatenate(parts, axis=1)
        return y if pitch is None else (y + roll_lanes(y, -pitch)) * 0.25

    fields = [ext[f] for f in range(4)]
    stores = (level0, level1, level2)
    for level in range(3):
        pitch = 2**level
        keep = stores[level]
        faces = coefficients(fields[3], fields[2], level, pitch)
        for j in range(5):
            keep[j] = faces[j]
        residuals = []
        for c in range(2):
            iterate = fields[c] * faces[4]
            keep[5 + c] = fields[c]
            residuals.append(residual_of(fields[c], iterate, faces, pitch))
        if level < 2:
            fields = [
                pool(x, i, pitch) for i, x in enumerate((*residuals, fields[2], fields[3]))
            ]

    first = HALO // 4
    for c in range(2):
        padded[c * 48 + 16 : c * 48 + 32, :] = pool(residuals[c][:, 0:128], c, None, first, 16)
    lanes16 = iota((16, 128), 1)
    pick = jnp.where(
        (lanes16 // 8 == iota((16, 128), 0)) & (lanes16 % 4 == 0), 0.25, 0.0
    )
    block[...] = exact_dot(pick, padded[...], True)
    copies3 = [
        send(block, block_halo.at[i], send3, recv3, i, da, db)
        for i, (da, db) in enumerate(DIRECTIONS)
    ]

    def assembled(mine, theirs, fill, masks):
        lanes = iota((16, 128), 1)
        parts = [jnp.full((8, 128), fill, F32)]
        for db in (-1, 0, 1):
            above = theirs(SOURCE_OF[(1, -db)])
            below = theirs(SOURCE_OF[(-1, -db)])
            here = mine if db == 0 else theirs(SOURCE_OF[(0, -db)])
            if masks:
                above, below = above * inside_up, below * inside_down
            part = here + roll_lanes(above, -16) + roll_lanes(below, 16)
            if masks and db != 0:
                part = part * (inside_left if db < 0 else inside_right)
            parts.append(jnp.where(lanes < 96, part, fill))
        parts.append(jnp.full((8, 128), fill, F32))
        return jnp.concatenate(parts, axis=0)

    for copy in copies2:
        copy.wait()
    reaction = assembled(coef_block[0], lambda i: coef_halo[i, 0], 1.0, False)
    viscous = assembled(coef_block[1], lambda i: coef_halo[i, 1], 0.0, True)
    mid_faces = []
    for level in range(3, 6):
        pitch = 2 ** (level - 3)
        mid_faces.append(coefficients(viscous, reaction, level, pitch))
        reaction, viscous = pool(reaction, 2, pitch), pool(viscous, 3, pitch)

    def level6_row(x):
        lanes = iota((8, 128), 1)
        total = jnp.zeros((8, 128), F32)
        for c in range(2):
            for r in range(2):
                here = c * 48 + 16 + 8 * r
                there = 2 * a + (c * 32 + r - here + 128)
                only = jnp.where(lanes == here, x, 0.0)
                total = total + pltpu.roll(only, lax.rem(there, 128), axis=1)
        return total[3:4] + roll_lanes(total[4:5], 64)

    def gather(slots, index, axis, sem):
        count = gx_count if axis == "gx" else gy_count

        def copy_to(k):
            peer = (lax.rem(a + k, count), b) if axis == "gx" else (a, lax.rem(b + k, count))
            return pltpu.make_async_remote_copy(
                src_ref=slots.at[index],
                dst_ref=slots.at[index],
                send_sem=gather_send.at[sem],
                recv_sem=gather_recv.at[sem],
                device_id=peer,
                device_id_type=MESH,
            )

        def start(k, carry):
            copy_to(k).start()
            return carry

        lax.fori_loop(1, count, start, 0)

    def gathered(slots, axis, sem):
        count = gx_count if axis == "gx" else gy_count
        every = pltpu.make_async_remote_copy(
            src_ref=slots.at[pl.ds(0, count - 1)],
            dst_ref=slots.at[pl.ds(0, count - 1)],
            send_sem=gather_send.at[sem],
            recv_sem=gather_recv.at[sem],
            device_id=at(1, 0),
            device_id_type=MESH,
        )
        every.wait()

    gx_coef[a, 0:1, :] = level6_row(reaction)
    gx_coef[a, 1:2, :] = level6_row(viscous)
    gather(gx_coef, a, "gx", 0)
    gathered(gx_coef, "gx", 0)
    gy_coef[b] = jnp.sum(gx_coef[...], axis=0)
    gather(gy_coef, b, "gy", 1)

    for copy in copies3:
        copy.wait()
    sources = []
    source = assembled(block[...], lambda i: block_halo[i], 0.0, False)
    for level in range(3, 6):
        pitch = 2 ** (level - 3)
        faces = mid_faces[level - 3]
        sources.append(source)
        source = pool(residual_of(source, source * faces[4], faces, pitch), 0, pitch)

    gx_source[a] = level6_row(source)
    gather(gx_source, a, "gx", 2)

    def spread_rows(x):
        n = x.shape[0]
        parts = []
        for t in range(x.shape[1] // 128):
            piece = x[:, t * 128 : t * 128 + 128]
            spread[t, pl.ds(0, n, stride=2), :] = piece
            spread[t, pl.ds(1, n, stride=2), :] = piece
            parts.append(spread[t, 0 : 2 * n, :])
        return parts[0] if len(parts) == 1 else jnp.concatenate(parts, axis=1)

    def widened(x, pitch):
        odd = (iota((1, x.shape[1]), 1) & pitch) != 0
        return spread_rows(jnp.where(odd, roll_lanes(x, pitch), x))

    cols6 = 64

    def whole(read, i):
        for j in range(gy_count):
            row = read(j)
            coarse[i, 2 * j : 2 * j + 1, :] = row
            coarse[i, 2 * j + 1 : 2 * j + 2, :] = roll_lanes(row, 64)
        return coarse[i]

    if gy_count * 2 < cols6:
        coarse[...] = jnp.zeros_like(coarse)

    def solved_coefficients():
        gathered(gy_coef, "gy", 1)
        reaction = whole(lambda j: gy_coef[j, 0:1, :], 0)
        viscous = whole(lambda j: gy_coef[j, 1:2, :], 1)
        if gx_count * 2 < 32 or gy_count * 2 < cols6:
            reaction = jnp.where(reaction == 0.0, 1.0, reaction)
        result = []
        for level in range(6, 9):
            pitch = 2 ** (level - 6)
            n = viscous.shape[0]
            closed = (iota((n, 128), 0) == 0, iota((n, 128), 1) % 32 < pitch)
            faces = coefficients(viscous, reaction, level, pitch, closed)
            down = jnp.where(iota((n, 128), 0) == n - 1, 0.0, faces[1])
            result.append((faces[0], down, *faces[2:]))
            if level < 8:
                reaction, viscous = pool(reaction, 2, pitch), pool(viscous, 3, pitch)
        return result

    gathered(gx_source, "gx", 2)
    gy_source[b] = jnp.sum(gx_source[...], axis=0)
    gather(gy_source, b, "gy", 3)
    coarse_faces = solved_coefficients()

    col6 = iota((16, 64), 1)
    take_cols = jnp.where(col6 == 2 * b - 3 + iota((16, 64), 0) // 2, 1.0, 0.0)
    to_lane = iota((128, 128), 1)
    second = to_lane >= 48
    local_lane = jnp.where(second, to_lane - 48, to_lane)
    from_lane = jnp.where(second, 32, 0) + 2 * a - 2 + local_lane // 8
    take_rows = jnp.where((iota((128, 128), 0) == from_lane) & (to_lane < 96), 1.0, 0.0)
    row2 = iota((80, 128), 0)
    comp2 = row2 // 40
    wanted = comp2 * 48 + 16 + (row2 - comp2 * 40 + 4) // 2 - 4
    rows_back = jnp.where(iota((80, 128), 1) == wanted, 1.0, 0.0)
    fine = iota((64, 256), 1)
    fine = jnp.where(fine < 192, fine, fine - 256) + 256
    cols_back = jnp.where(iota((64, 256), 0) == 24 + fine // 8 - 32, 1.0, 0.0)

    gathered(gy_source, "gy", 3)
    source = whole(lambda j: gy_source[j], 2)
    coarse_sources = []
    for level in range(6, 8):
        pitch = 2 ** (level - 6)
        faces = coarse_faces[level - 6]
        coarse_sources.append(source)
        source = pool(residual_of(source, source * faces[4], faces, pitch), 0, pitch)
    up, down, left, right, weight = coarse_faces[2]
    scaled = (weight * up, weight * down, weight * left, weight * right)
    start = weight * source
    solution_now = start
    for _ in range(7):
        solution_now = (KEEP * solution_now + start) + inflow(solution_now, scaled, 4)
    for level in (7, 6):
        pitch = 2 ** (level - 6)
        faces = coarse_faces[level - 6]
        source = coarse_sources[level - 6]
        iterate = source * faces[4] + widened(solution_now, pitch)
        solution_now = swept(source, iterate, faces, pitch)

    correction = exact_dot(exact_dot(take_cols, solution_now), take_rows)
    for level in (5, 4, 3):
        pitch = 2 ** (level - 3)
        faces = mid_faces[level - 3]
        source = sources[level - 3]
        if level < 5:
            correction = widened(correction, pitch)
        correction = swept(source, source * faces[4] + correction, faces, pitch)

    both = exact_dot(exact_dot(rows_back, correction, True), cols_back)
    fine_now = [both[0:40], both[40:80]]
    for level in (2, 1, 0):
        pitch = 2**level
        keep = stores[level]
        faces = [keep[j] for j in range(5)]
        for c in range(2):
            source = keep[5 + c]
            correction = fine_now[c] if level == 2 else widened(fine_now[c], pitch)
            result = swept(source, source * faces[4] + correction, faces, pitch)
            if level == 0:
                out_ref[c] = result[HALO : HALO + TILE, 0:128]
            else:
                fine_now[c] = result


def solution(mesh):
    gx_count, gy_count = mesh.shape["gx"], mesh.shape["gy"]

    def per_device(right_side, shift_coef, viscosity, wet_tiles):
        hbm = pl.BlockSpec(memory_space=pl.ANY)
        dma = pltpu.SemaphoreType.DMA
        return pl.pallas_call(
            functools.partial(kernel, gx_count, gy_count),
            out_shape=jax.ShapeDtypeStruct((2, TILE, TILE), F32),
            in_specs=[hbm, hbm, hbm, pl.BlockSpec(memory_space=pltpu.SMEM)],
            out_specs=pl.BlockSpec(memory_space=pltpu.VMEM),
            scratch_shapes=[
                pltpu.VMEM((4, TILE, TILE), F32),
                pltpu.VMEM((2, 64, 128), F32),
                pltpu.VMEM((2, 16, 128), F32),
                pltpu.VMEM((2, 4, HALO, 128), F32),
                pltpu.VMEM((2, 64, 128), F32),
                pltpu.VMEM((4, HALO, 128), F32),
                pltpu.VMEM((8, 2, 16, 128), F32),
                pltpu.VMEM((16, 128), F32),
                pltpu.VMEM((8, 16, 128), F32),
                pltpu.VMEM((gx_count, 2, 128), F32),
                pltpu.VMEM((gx_count, 1, 128), F32),
                pltpu.VMEM((gy_count, 2, 128), F32),
                pltpu.VMEM((gy_count, 1, 128), F32),
                pltpu.VMEM((4, ROWS, 256), F32),
                pltpu.VMEM((4, 2, ROWS, 128), F32),
                pltpu.VMEM((7, ROWS, 256), F32),
                pltpu.VMEM((7, ROWS // 2, 256), F32),
                pltpu.VMEM((7, ROWS // 4, 256), F32),
                pltpu.VMEM((128, 128), F32),
                pltpu.VMEM((2, ROWS, 128), F32),
                pltpu.VMEM((3, 64, 128), F32),
                dma((3,)),
                dma((8,)),
                dma((8,)),
                dma((8,)),
                dma((8,)),
                dma((8,)),
                dma((8,)),
                dma((4,)),
                dma((4,)),
            ],
            compiler_params=pltpu.CompilerParams(collective_id=0, has_side_effects=True),
            name="vcycle",
        )(right_side, shift_coef, viscosity, wet_tiles)

    placed = (P(None, "gx", "gy"), P("gx", "gy"), P("gx", "gy"), P("gx", "gy"))
    return jax.shard_map(
        per_device, mesh=mesh, in_specs=placed, out_specs=P(None, "gx", "gy"), check_vma=False
    )
```

```python
import functools

import jax
import jax.numpy as jnp
from jax import lax
from jax.experimental import pallas as pl
from jax.experimental.pallas import tpu as pltpu
from jax.sharding import PartitionSpec as P

TILE = 128
OMEGA = 0.8
KEEP = 1.0 - OMEGA
HALO = 24
ROWS = TILE + 2 * HALO
PAD = 8
F32 = jnp.float32
MESH = pl.DeviceIdType.MESH
DIRECTIONS = ((-1, 0), (1, 0), (0, -1), (0, 1), (-1, -1), (-1, 1), (1, -1), (1, 1))


def iota(shape, dim):
    return lax.broadcasted_iota(jnp.int32, shape, dim)


def roll_rows(x, k):
    return pltpu.roll(x, k % x.shape[0], axis=0)


def roll_lanes(x, k):
    return pltpu.roll(x, k % x.shape[1], axis=1)


def exact_dot(a, b, transposed=False):
    dims = (((1,), (1,)), ((), ())) if transposed else (((1,), (0,)), ((), ()))
    return lax.dot_general(
        a, b, dims, precision=lax.Precision.HIGHEST, preferred_element_type=F32
    )


def coefficients(viscous, reaction, level, pitch, closed=None):
    spacing = 0.25**level
    up = jnp.minimum(viscous, roll_rows(viscous, 1)) * spacing
    left = jnp.minimum(viscous, roll_lanes(viscous, pitch)) * spacing
    if closed is not None:
        up = jnp.where(closed[0], 0.0, up)
        left = jnp.where(closed[1], 0.0, left)
    down = roll_rows(up, -1)
    right = roll_lanes(left, -pitch)
    weight = OMEGA / (reaction + ((up + down) + (left + right)))
    return up, down, left, right, weight


def inflow(iterate, faces, pitch):
    up, down, left, right = faces[:4]
    return (up * roll_rows(iterate, 1) + down * roll_rows(iterate, -1)) + (
        left * roll_lanes(iterate, pitch) + right * roll_lanes(iterate, -pitch)
    )


def residual_of(source, iterate, faces, pitch):
    return KEEP * source + inflow(iterate, faces, pitch)


def swept(source, iterate, faces, pitch):
    return KEEP * iterate + faces[4] * (source + inflow(iterate, faces, pitch))


def kernel(
    gx_count,
    gy_count,
    rhs_hbm,
    shift_hbm,
    visc_hbm,
    wet_hbm,
    out_ref,
    own,
    wet_ref,
    strips,
    row_halo,
    col_halo,
    corner_halo,
    column_coef,
    column_source,
    gy_coef,
    gy_source,
    ext,
    pooled,
    level0,
    level1,
    level2,
    level3,
    stacked,
    spread,
    coarse,
    load_sem,
    halo_send,
    halo_recv,
    coef_send,
    coef_recv,
    source_send,
    source_recv,
    gather_send,
    gather_recv,
):
    a = lax.axis_index("gx")
    b = lax.axis_index("gy")
    has_up, has_down = a > 0, a < gx_count - 1
    has_left, has_right = b > 0, b < gy_count - 1
    has_row = {-1: has_up, 1: has_down}
    has_col = {-1: has_left, 1: has_right}

    def exists(da, db):
        if da == 0:
            return has_col[db]
        if db == 0:
            return has_row[da]
        return jnp.logical_and(has_row[da], has_col[db])

    loads = [
        pltpu.make_async_copy(wet_hbm, wet_ref, load_sem.at[3]),
        pltpu.make_async_copy(visc_hbm, own.at[3], load_sem.at[2]),
        pltpu.make_async_copy(rhs_hbm, own.at[pl.ds(0, 2)], load_sem.at[0]),
        pltpu.make_async_copy(shift_hbm, own.at[2], load_sem.at[1]),
    ]
    for load in loads:
        load.start()

    barrier = pltpu.get_barrier_semaphore()

    def greet(da, db):
        peer = (lax.rem(a + da, gx_count), lax.rem(b + db + gy_count, gy_count))
        pl.semaphore_signal(barrier, inc=1, device_id=peer, device_id_type=MESH)

    def greet_column(db):
        def one(k, carry):
            greet(k, db)
            return carry

        lax.fori_loop(1, gx_count, one, 0)

    def greet_row(k, carry):
        greet(0, k)
        return carry

    pl.when(has_left)(lambda: greet_column(-1))
    pl.when(has_right)(lambda: greet_column(1))
    greet_column(0)
    lax.fori_loop(1, gy_count, greet_row, 0)

    for f in range(4):
        for t in range(2):
            edge = jnp.full((PAD, 128), 1.0 if f == 2 else 0.0, F32)
            pooled[f, t, 0:PAD, :] = edge
            pooled[f, t, PAD + ROWS :, :] = edge
    for load in loads:
        load.wait()

    wet = wet_ref[0, 0].astype(F32)
    for f in (0, 1, 3):
        own[f] = own[f] * wet

    slot = iota((TILE, 128), 1) // 32
    for side, first in ((0, 0), (1, TILE - HALO)):
        packed = roll_lanes(own[0], -first)
        for f in range(1, 4):
            packed = jnp.where(slot == f, roll_lanes(own[f], f * 32 - first), packed)
        strips[side] = packed

    columns = jnp.where(has_left, 1, 0) + jnp.where(has_right, 1, 0) + 1
    pl.semaphore_wait(barrier, columns * (gx_count - 1) + gy_count - 1)

    def remote(src, dst, send_sem, recv_sem, da, db):
        peer = (lax.rem(a + da + gx_count, gx_count), lax.rem(b + db + gy_count, gy_count))
        return pltpu.make_async_remote_copy(
            src_ref=src,
            dst_ref=dst,
            send_sem=send_sem,
            recv_sem=recv_sem,
            device_id=peer,
            device_id_type=MESH,
        )

    halo_copies = []
    for i, (da, db) in enumerate(DIRECTIONS):
        first = 0 if da < 0 else TILE - HALO
        if db == 0:
            src, dst = own.at[:, pl.ds(first, HALO)], row_halo.at[i]
        elif da == 0:
            src, dst = strips.at[0 if db < 0 else 1], col_halo.at[i - 2]
        else:
            src = strips.at[0 if db < 0 else 1, pl.ds(first, HALO)]
            dst = corner_halo.at[i - 4]
        copy = remote(src, dst, halo_send.at[i], halo_recv.at[i], da, db)
        halo_copies.append(copy)
    for i in (4, 5, 6, 7, 2, 3, 0, 1):
        pl.when(exists(*DIRECTIONS[i]))(halo_copies[i].start)

    gx_order = sorted(range(1, gx_count), key=lambda k: -min(k, gx_count - k))

    def column_copies(slots, sends, recvs, db):
        def copy(k):
            return remote(
                slots.at[1, a], slots.at[1 - db, a], sends.at[db + 1], recvs.at[1 - db], k, db
            )

        ks = gx_order if db == 0 else [*gx_order, 0]
        return [copy(k) for k in ks]

    def start_columns(slots, sends, recvs):
        for db in (-1, 1, 0):
            copies = column_copies(slots, sends, recvs, db)

            def start(copies=copies):
                for copy in copies:
                    copy.start()

            if db == 0:
                start()
            else:
                pl.when(has_col[db])(start)

    def finish_columns(slots, sends, recvs):
        for db in (-1, 1, 0):
            count = gx_count - 1 if db == 0 else gx_count
            every = remote(
                slots.at[1 - db, pl.ds(0, count)],
                slots.at[1 - db, pl.ds(0, count)],
                sends.at[db + 1],
                recvs.at[1 + db],
                1,
                0,
            )
            if db == 0:
                every.wait()
            else:
                pl.when(has_col[db])(every.wait)

    lane8 = iota((8, 128), 1)
    own_column = lane8 // 16 == iota((8, 128), 0)
    average = jnp.where(own_column, 0.0625, 0.0)
    to_lane = iota((128, 128), 1)
    from_row = iota((128, 128), 0)
    total = jnp.zeros((8, 128), F32)
    for f in range(2):
        to_row = jnp.where(
            (from_row // 16 == to_lane % 8) & (to_lane // 8 % 2 == f), 0.0625, 0.0
        )
        total = total + exact_dot(exact_dot(average, own[2 + f], True), to_row)

    def one_row(x):
        mine = jnp.where(lane8 // 16 == 7 - iota((8, 128), 0), x, 0.0)
        turned = pltpu.roll(mine, lax.rem(8 * a + 8, 128), axis=1)
        return jnp.sum(turned, axis=0, keepdims=True)

    column_coef[1, a] = one_row(total)
    start_columns(column_coef, coef_send, coef_recv)

    for f in range(4):
        ext[f, HALO : HALO + TILE, 0:128] = own[f]
    for i, (da, db) in enumerate(DIRECTIONS):
        pl.when(exists(da, db))(halo_copies[i].wait_send)
        pl.when(exists(-da, -db))(halo_copies[i].wait_recv)

    lane = iota((1, 128), 1)
    all_up = lane < jnp.where(has_up, 128, 0)
    all_down = lane < jnp.where(has_down, 128, 0)
    beside = (lane < jnp.where(has_right, HALO, 0)) | (
        lane >= jnp.where(has_left, TILE - HALO, 128)
    )
    for f in range(4):
        fill = 1.0 if f == 2 else 0.0
        ext[f, 0:HALO, 0:128] = jnp.where(all_up, row_halo[1, f], fill)
        ext[f, HALO + TILE :, 0:128] = jnp.where(all_down, row_halo[0, f], fill)

        def side(right, left, valid):
            r = roll_lanes(right, -f * 32)
            l = roll_lanes(left, TILE - HALO - f * 32)
            return jnp.where(valid, jnp.where(lane < 64, r, l), fill)

        ext[f, HALO : HALO + TILE, 128:256] = side(col_halo[0], col_halo[1], beside)
        ext[f, 0:HALO, 128:256] = side(corner_halo[2], corner_halo[3], beside & all_up)
        ext[f, HALO + TILE :, 128:256] = side(corner_halo[0], corner_halo[1], beside & all_down)

    def pool(x, i, pitch, first=0, start=0, rows=None):
        n = x.shape[0]
        width = x.shape[1]
        rows = n // 2 if rows is None else rows
        parts = []
        for t in range(width // 128):
            pooled[i, t, first : first + n, :] = x[:, t * 128 : t * 128 + 128]
            parts.append(
                pooled[i, t, pl.ds(start, rows, stride=2), :]
                + pooled[i, t, pl.ds(start + 1, rows, stride=2), :]
            )
        y = parts[0] if len(parts) == 1 else jnp.concatenate(parts, axis=1)
        return y if pitch is None else (y + roll_lanes(y, -pitch)) * 0.25

    fields = [ext[f] for f in range(4)]
    stores = (level0, level1, level2, level3)
    for level in range(4):
        pitch = 2**level
        keep = stores[level]
        faces = coefficients(fields[3], fields[2], level, pitch)
        for j in range(5):
            keep[j] = faces[j]
        residuals = []
        for c in range(2):
            iterate = fields[c] * faces[4]
            keep[5 + c] = fields[c]
            residuals.append(residual_of(fields[c], iterate, faces, pitch))
        if level < 3:
            shape = (PAD, 0, (ROWS + 2 * PAD) // 2) if level == 0 else (0, 0, None)
            fields = [
                pool(x, i, pitch, *shape)
                for i, x in enumerate((*residuals, fields[2], fields[3]))
            ]

    for c in range(2):
        half = pool(residuals[c][:, 0:128], c, None, 0, 4, 8)
        for j in range(8):
            stacked[j * 16 + c * 8 : j * 16 + c * 8 + 8, :] = half
    pick = jnp.where(own_column & (lane8 % 8 == 0), 0.25, 0.0)
    column_source[1, a] = one_row(exact_dot(pick, stacked[...], True))
    start_columns(column_source, source_send, source_recv)

    def assembled(slots, fills):
        parts = ([], [])
        for col in range(3):
            for t in range(2):
                block = jnp.zeros((8, 128), F32)
                for j in range(gx_count):
                    row = jnp.broadcast_to(slots[col, j], (8, 128))
                    moved = pltpu.roll(
                        row, 8 - t * 8, axis=1, stride=16, stride_axis=0
                    )
                    block = jnp.where(lane8 // 8 == j, moved, block)
                if gx_count < 16:
                    block = jnp.where(lane8 // 8 < gx_count, block, fills[t])
                if col != 1:
                    limit = jnp.where(has_left if col == 0 else has_right, 128, 0)
                    block = jnp.where(lane8 < limit, block, fills[t])
                parts[t].append(block)
        return [
            jnp.concatenate([*parts[t], jnp.full((8, 128), fills[t], F32)], axis=0)
            for t in range(2)
        ]

    def closed_rows(shape, pitch, columns_too):
        first_col = iota(shape, 0) == (0 if columns_too else -1)
        return first_col, iota(shape, 1) < pitch

    finish_columns(column_coef, coef_send, coef_recv)
    reaction, viscous = assembled(column_coef, (1.0, 0.0))
    mid_faces = []
    for level in (4, 5):
        pitch = 2 ** (level - 4)
        closed = closed_rows(viscous.shape, pitch, False)
        mid_faces.append(coefficients(viscous, reaction, level, pitch, closed))
        reaction, viscous = pool(reaction, 2, pitch), pool(viscous, 3, pitch)

    def level6_row(x, y):
        x, y = jnp.where(lane8 % 4 == 0, x, 0.0), jnp.where(lane8 % 4 == 0, y, 0.0)
        both = x + roll_lanes(y, 1)
        return both[2:3] + roll_lanes(both[3:4], 2)

    def hops(k):
        x, y = k // 8, k % 8
        return min(x, 4 - x) + min(y, 8 - y)

    gy_order = sorted(range(1, gy_count), key=lambda k: -hops(k))

    def start_row(slots, sem):
        for k in gy_order:
            remote(slots.at[b], slots.at[b], gather_send.at[sem], gather_recv.at[sem], 0, k).start()

    def finish_row(slots, sem):
        rest = slots.at[pl.ds(0, gy_count - 1)]
        remote(rest, rest, gather_send.at[sem], gather_recv.at[sem], 0, 1).wait()

    gy_coef[b, 0:1, :] = level6_row(reaction, reaction)
    gy_coef[b, 1:2, :] = level6_row(viscous, viscous)
    start_row(gy_coef, 0)

    finish_columns(column_source, source_send, source_recv)
    source4 = assembled(column_source, (0.0, 0.0))
    source5 = [
        pool(residual_of(x, x * mid_faces[0][4], mid_faces[0], 1), c, 1)
        for c, x in enumerate(source4)
    ]
    source6 = [
        pool(residual_of(x, x * mid_faces[1][4], mid_faces[1], 2), c, 2)
        for c, x in enumerate(source5)
    ]
    gy_source[b] = level6_row(*source6)
    start_row(gy_source, 1)

    def spread_rows(x, i=0):
        n = x.shape[0]
        parts = []
        for t in range(x.shape[1] // 128):
            piece = x[:, t * 128 : t * 128 + 128]
            spread[i, t, pl.ds(0, n, stride=2), :] = piece
            spread[i, t, pl.ds(1, n, stride=2), :] = piece
            start = PAD if 2 * n > ROWS else 0
            parts.append(spread[i, t, start : 2 * n - start, :])
        return parts[0] if len(parts) == 1 else jnp.concatenate(parts, axis=1)

    def widened(x, pitch, i=0):
        odd = (iota((1, x.shape[1]), 1) & pitch) != 0
        return spread_rows(jnp.where(odd, roll_lanes(x, pitch), x), i)

    cols6 = 64

    def whole(read, i):
        for j in range(gy_count):
            coarse[i, 64 + j : 65 + j, :] = read(j)
        rows = coarse[i, 64:96, :]
        coarse[i, pl.ds(0, 32, stride=2), :] = rows
        coarse[i, pl.ds(1, 32, stride=2), :] = roll_lanes(rows, -2)
        return coarse[i, 0:cols6, :]

    if gy_count * 2 < cols6:
        coarse[...] = jnp.zeros_like(coarse)

    finish_row(gy_coef, 0)
    reaction = whole(lambda j: gy_coef[j, 0:1, :], 0)
    viscous = whole(lambda j: gy_coef[j, 1:2, :], 1)
    if gx_count * 2 < 32 or gy_count * 2 < cols6:
        reaction = jnp.where(reaction == 0.0, 1.0, reaction)
    coarse_faces = []
    for level in range(6, 9):
        pitch = 2 ** (level - 4)
        closed = closed_rows(viscous.shape, pitch, True)
        coarse_faces.append(coefficients(viscous, reaction, level, pitch, closed))
        if level < 8:
            reaction, viscous = pool(reaction, 2, pitch), pool(viscous, 3, pitch)
    up, down, left, right, weight8 = coarse_faces[2]
    scaled8 = (weight8 * up, weight8 * down, weight8 * left, weight8 * right)

    take_cols = jnp.where(
        iota((16, cols6), 1) == 2 * b - 2 + iota((16, cols6), 0) // 2, 1.0, 0.0
    )
    rows_back = jnp.where(
        iota((24, 128), 1) == 8 * a + (iota((24, 128), 0) + 4) // 2 - 4, 1.0, 0.0
    )
    fine = iota((32, 256), 1)
    fine = jnp.where(fine < 192, fine + 256, fine)
    cols_back = jnp.where(iota((32, 256), 0) == fine // 16 - 8, 1.0, 0.0)

    finish_row(gy_source, 1)
    source = whole(lambda j: gy_source[j], 2)
    coarse_sources = []
    for level in (6, 7):
        pitch = 2 ** (level - 4)
        faces = coarse_faces[level - 6]
        coarse_sources.append(source)
        source = pool(residual_of(source, source * faces[4], faces, pitch), 0, pitch)
    start = weight8 * source
    now = start
    for _ in range(7):
        now = (KEEP * now + start) + inflow(now, scaled8, 16)
    for level in (7, 6):
        pitch = 2 ** (level - 4)
        faces = coarse_faces[level - 6]
        source = coarse_sources[level - 6]
        now = swept(source, source * faces[4] + widened(now, pitch), faces, pitch)

    near = exact_dot(take_cols, now)
    lane16 = iota((16, 128), 1)
    current = []
    for c in range(2):
        mine = jnp.where(lane16 % 4 == c, near, 0.0)
        mine = roll_lanes(mine, -c) if c else mine
        correction = mine + roll_lanes(mine, 2)
        x = source5[c]
        result = swept(x, x * mid_faces[1][4] + correction, mid_faces[1], 2)
        x = source4[c]
        result = swept(x, x * mid_faces[0][4] + widened(result, 1, c), mid_faces[0], 1)
        current.append(exact_dot(exact_dot(rows_back, result, True), cols_back))

    for level in (3, 2, 1, 0):
        pitch = 2**level
        keep = stores[level]
        faces = [keep[j] for j in range(5)]
        for c in range(2):
            source = keep[5 + c]
            correction = current[c] if level == 3 else widened(current[c], pitch, c)
            result = swept(source, source * faces[4] + correction, faces, pitch)
            if level == 0:
                out_ref[c] = result[HALO : HALO + TILE, 0:128]
            else:
                current[c] = result


def solution(mesh):
    gx_count, gy_count = mesh.shape["gx"], mesh.shape["gy"]

    def per_device(right_side, shift_coef, viscosity, wet_tiles):
        hbm = pl.BlockSpec(memory_space=pltpu.HBM)
        dma = pltpu.SemaphoreType.DMA
        inner = (ROWS + 2 * PAD) // 2
        return pl.pallas_call(
            functools.partial(kernel, gx_count, gy_count),
            out_shape=pltpu.VMEM((2, TILE, TILE), F32),
            in_specs=[hbm, hbm, hbm, hbm],
            out_specs=pl.BlockSpec(memory_space=pltpu.VMEM),
            scratch_shapes=[
                pltpu.VMEM((4, TILE, TILE), F32),
                pltpu.SMEM((1, 1), jnp.int32),
                pltpu.VMEM((2, TILE, 128), F32),
                pltpu.VMEM((2, 4, HALO, 128), F32),
                pltpu.VMEM((2, TILE, 128), F32),
                pltpu.VMEM((4, HALO, 128), F32),
                pltpu.VMEM((3, gx_count, 1, 128), F32),
                pltpu.VMEM((3, gx_count, 1, 128), F32),
                pltpu.VMEM((gy_count, 2, 128), F32),
                pltpu.VMEM((gy_count, 1, 128), F32),
                pltpu.VMEM((4, ROWS, 256), F32),
                pltpu.VMEM((4, 2, ROWS + 2 * PAD, 128), F32),
                pltpu.VMEM((7, ROWS, 256), F32),
                pltpu.VMEM((7, inner, 256), F32),
                pltpu.VMEM((7, inner // 2, 256), F32),
                pltpu.VMEM((7, inner // 4, 256), F32),
                pltpu.VMEM((128, 128), F32),
                pltpu.VMEM((2, 2, ROWS + 2 * PAD, 128), F32),
                pltpu.VMEM((3, 96, 128), F32),
                dma((4,)),
                dma((8,)),
                dma((8,)),
                dma((3,)),
                dma((3,)),
                dma((3,)),
                dma((3,)),
                dma((2,)),
                dma((2,)),
            ],
            compiler_params=pltpu.CompilerParams(collective_id=0, has_side_effects=True),
            name="vcycle",
        )(right_side, shift_coef, viscosity, wet_tiles)

    placed = (P(None, "gx", "gy"), P("gx", "gy"), P("gx", "gy"), P("gx", "gy"))
    return jax.shard_map(
        per_device, mesh=mesh, in_specs=placed, out_specs=P(None, "gx", "gy"), check_vma=False
    )
```

```python
import functools

import jax
import jax.numpy as jnp
from jax import lax
from jax.experimental import pallas as pl
from jax.experimental.pallas import tpu as pltpu
from jax.sharding import PartitionSpec as P

TILE = 128
OMEGA = 0.8
KEEP = 1.0 - OMEGA
HALO = 24
ROWS = TILE + 2 * HALO
PAD = 8
F32 = jnp.float32
MESH = pl.DeviceIdType.MESH
DIRECTIONS = ((-1, 0), (1, 0), (0, -1), (0, 1), (-1, -1), (-1, 1), (1, -1), (1, 1))


def iota(shape, dim):
    return lax.broadcasted_iota(jnp.int32, shape, dim)


def roll_rows(x, k):
    return pltpu.roll(x, k % x.shape[0], axis=0)


def roll_lanes(x, k):
    return pltpu.roll(x, k % x.shape[1], axis=1)


def exact_dot(a, b, transposed=False):
    dims = (((1,), (1,)), ((), ())) if transposed else (((1,), (0,)), ((), ()))
    return lax.dot_general(
        a, b, dims, precision=lax.Precision.HIGHEST, preferred_element_type=F32
    )


def coefficients(viscous, reaction, level, pitch, closed=None):
    spacing = 0.25**level
    up = jnp.minimum(viscous, roll_rows(viscous, 1)) * spacing
    left = jnp.minimum(viscous, roll_lanes(viscous, pitch)) * spacing
    if closed is not None:
        up = jnp.where(closed[0], 0.0, up)
        left = jnp.where(closed[1], 0.0, left)
    down = roll_rows(up, -1)
    right = roll_lanes(left, -pitch)
    weight = OMEGA / (reaction + ((up + down) + (left + right)))
    return up, down, left, right, weight


def inflow(iterate, faces, pitch):
    up, down, left, right = faces[:4]
    return (up * roll_rows(iterate, 1) + down * roll_rows(iterate, -1)) + (
        left * roll_lanes(iterate, pitch) + right * roll_lanes(iterate, -pitch)
    )


def residual_of(source, iterate, faces, pitch):
    return KEEP * source + inflow(iterate, faces, pitch)


def swept(source, iterate, faces, pitch):
    return KEEP * iterate + faces[4] * (source + inflow(iterate, faces, pitch))


def kernel(
    gx_count,
    gy_count,
    rhs_hbm,
    shift_hbm,
    visc_hbm,
    wet_hbm,
    out_ref,
    own,
    wet_ref,
    strips,
    row_halo,
    col_halo,
    corner_halo,
    column_coef,
    column_source,
    gy_coef,
    gy_source,
    ext,
    pooled,
    level0,
    level1,
    level2,
    level3,
    stacked,
    spread,
    coarse,
    load_sem,
    halo_send,
    halo_recv,
    coef_send,
    coef_recv,
    source_send,
    source_recv,
    gather_send,
    gather_recv,
    known,
):
    a = lax.axis_index("gx")
    b = lax.axis_index("gy")
    has_up, has_down = a > 0, a < gx_count - 1
    has_left, has_right = b > 0, b < gy_count - 1
    has_row = {-1: has_up, 1: has_down}
    has_col = {-1: has_left, 1: has_right}

    def exists(da, db):
        if da == 0:
            return has_col[db]
        if db == 0:
            return has_row[da]
        return jnp.logical_and(has_row[da], has_col[db])

    barrier = pltpu.get_barrier_semaphore()

    def around(da, db):
        return (lax.rem(a + da + gx_count, gx_count), lax.rem(b + db + gy_count, gy_count))

    for da, db in DIRECTIONS[4:] + DIRECTIONS[:4]:
        pl.semaphore_signal(barrier, inc=1, device_id=around(da, db), device_id_type=MESH)

    loads = [
        pltpu.make_async_copy(wet_hbm, wet_ref, load_sem.at[3]),
        pltpu.make_async_copy(visc_hbm, own.at[3], load_sem.at[2]),
        pltpu.make_async_copy(rhs_hbm, own.at[pl.ds(0, 2)], load_sem.at[0]),
        pltpu.make_async_copy(shift_hbm, own.at[2], load_sem.at[1]),
    ]
    for load in loads:
        load.start()

    reach = {"gx": 1, "gy": 1}

    def tell(axis):
        r, count = reach[axis], gx_count if axis == "gx" else gy_count
        if r < count // 2:
            sem = known.at[(0 if axis == "gx" else 8) + r.bit_length()]
            for step in (r, -r):
                peer = around(step, 0) if axis == "gx" else around(0, step)
                pl.semaphore_signal(sem, inc=1, device_id=peer, device_id_type=MESH)

    def hear(axis):
        r, count = reach[axis], gx_count if axis == "gx" else gy_count
        if r < count // 2:
            sem = known.at[(0 if axis == "gx" else 8) + r.bit_length()]
            pl.semaphore_wait(sem, 2)
            reach[axis] = 2 * r

    for f in range(4):
        for t in range(2):
            edge = jnp.full((PAD, 128), 1.0 if f == 2 else 0.0, F32)
            pooled[f, t, 0:PAD, :] = edge
            pooled[f, t, PAD + ROWS :, :] = edge
    for load in loads:
        load.wait()

    wet = wet_ref[0, 0].astype(F32)
    for f in (0, 1, 3):
        own[f] = own[f] * wet

    slot = iota((TILE, 128), 1) // 32
    for side, first in ((0, 0), (1, TILE - HALO)):
        packed = roll_lanes(own[0], -first)
        for f in range(1, 4):
            packed = jnp.where(slot == f, roll_lanes(own[f], f * 32 - first), packed)
        strips[side] = packed

    pl.semaphore_wait(barrier, 8)

    def remote(src, dst, send_sem, recv_sem, da, db):
        return pltpu.make_async_remote_copy(
            src_ref=src,
            dst_ref=dst,
            send_sem=send_sem,
            recv_sem=recv_sem,
            device_id=around(da, db),
            device_id_type=MESH,
        )

    halo_copies = []
    for i, (da, db) in enumerate(DIRECTIONS):
        first = 0 if da < 0 else TILE - HALO
        if db == 0:
            src, dst = own.at[:, pl.ds(first, HALO)], row_halo.at[i]
        elif da == 0:
            src, dst = strips.at[0 if db < 0 else 1], col_halo.at[i - 2]
        else:
            src = strips.at[0 if db < 0 else 1, pl.ds(first, HALO)]
            dst = corner_halo.at[i - 4]
        copy = remote(src, dst, halo_send.at[i], halo_recv.at[i], da, db)
        halo_copies.append(copy)
    for i in (4, 5, 6, 7, 2, 3, 0, 1):
        pl.when(exists(*DIRECTIONS[i]))(halo_copies[i].start)
    tell("gx")
    tell("gy")

    gx_order = sorted(range(1, gx_count), key=lambda k: -min(k, gx_count - k))

    def column_copies(slots, sends, recvs, db):
        def copy(k):
            return remote(
                slots.at[1, a], slots.at[1 - db, a], sends.at[db + 1], recvs.at[1 - db], k, db
            )

        ks = gx_order if db == 0 else [*gx_order, 0]
        return [copy(k) for k in ks]

    def start_columns(slots, sends, recvs):
        for db in (-1, 1, 0):
            copies = column_copies(slots, sends, recvs, db)

            def start(copies=copies):
                for copy in copies:
                    copy.start()

            if db == 0:
                start()
            else:
                pl.when(has_col[db])(start)

    def finish_columns(slots, sends, recvs):
        for db in (-1, 1, 0):
            count = gx_count - 1 if db == 0 else gx_count
            every = remote(
                slots.at[1 - db, pl.ds(0, count)],
                slots.at[1 - db, pl.ds(0, count)],
                sends.at[db + 1],
                recvs.at[1 + db],
                1,
                0,
            )
            if db == 0:
                every.wait()
            else:
                pl.when(has_col[db])(every.wait)

    lane8 = iota((8, 128), 1)
    own_column = lane8 // 16 == iota((8, 128), 0)
    average = jnp.where(own_column, 0.0625, 0.0)
    to_lane = iota((128, 128), 1)
    from_row = iota((128, 128), 0)
    total = jnp.zeros((8, 128), F32)
    for f in range(2):
        to_row = jnp.where(
            (from_row // 16 == to_lane % 8) & (to_lane // 8 % 2 == f), 0.0625, 0.0
        )
        total = total + exact_dot(exact_dot(average, own[2 + f], True), to_row)

    def one_row(x):
        mine = jnp.where(lane8 // 16 == 7 - iota((8, 128), 0), x, 0.0)
        turned = pltpu.roll(mine, lax.rem(8 * a + 8, 128), axis=1)
        return jnp.sum(turned, axis=0, keepdims=True)

    column_coef[1, a] = one_row(total)
    hear("gx")
    tell("gx")
    hear("gy")
    tell("gy")

    for f in range(4):
        ext[f, HALO : HALO + TILE, 0:128] = own[f]
    hear("gx")
    tell("gx")
    for i, (da, db) in enumerate(DIRECTIONS):
        pl.when(exists(da, db))(halo_copies[i].wait_send)
        pl.when(exists(-da, -db))(halo_copies[i].wait_recv)

    lane = iota((1, 128), 1)
    all_up = lane < jnp.where(has_up, 128, 0)
    all_down = lane < jnp.where(has_down, 128, 0)
    beside = (lane < jnp.where(has_right, HALO, 0)) | (
        lane >= jnp.where(has_left, TILE - HALO, 128)
    )
    for f in range(4):
        fill = 1.0 if f == 2 else 0.0
        ext[f, 0:HALO, 0:128] = jnp.where(all_up, row_halo[1, f], fill)
        ext[f, HALO + TILE :, 0:128] = jnp.where(all_down, row_halo[0, f], fill)

        def side(right, left, valid):
            r = roll_lanes(right, -f * 32)
            l = roll_lanes(left, TILE - HALO - f * 32)
            return jnp.where(valid, jnp.where(lane < 64, r, l), fill)

        ext[f, HALO : HALO + TILE, 128:256] = side(col_halo[0], col_halo[1], beside)
        ext[f, 0:HALO, 128:256] = side(corner_halo[2], corner_halo[3], beside & all_up)
        ext[f, HALO + TILE :, 128:256] = side(corner_halo[0], corner_halo[1], beside & all_down)

    def pool(x, i, pitch, first=0, start=0, rows=None):
        n = x.shape[0]
        width = x.shape[1]
        rows = n // 2 if rows is None else rows
        parts = []
        for t in range(width // 128):
            pooled[i, t, first : first + n, :] = x[:, t * 128 : t * 128 + 128]
            parts.append(
                pooled[i, t, pl.ds(start, rows, stride=2), :]
                + pooled[i, t, pl.ds(start + 1, rows, stride=2), :]
            )
        y = parts[0] if len(parts) == 1 else jnp.concatenate(parts, axis=1)
        return y if pitch is None else (y + roll_lanes(y, -pitch)) * 0.25

    fields = [ext[f] for f in range(4)]
    stores = (level0, level1, level2, level3)
    for level in range(4):
        pitch = 2**level
        keep = stores[level]
        faces = coefficients(fields[3], fields[2], level, pitch)
        for j in range(5):
            keep[j] = faces[j]
        residuals = []
        for c in range(2):
            iterate = fields[c] * faces[4]
            keep[5 + c] = fields[c]
            residuals.append(residual_of(fields[c], iterate, faces, pitch))
        if level == 0:
            hear("gy")
            tell("gy")
        if level == 1:
            hear("gx")
            assert reach["gx"] >= gx_count // 2
            start_columns(column_coef, coef_send, coef_recv)
        if level < 3:
            shape = (PAD, 0, (ROWS + 2 * PAD) // 2) if level == 0 else (0, 0, None)
            fields = [
                pool(x, i, pitch, *shape)
                for i, x in enumerate((*residuals, fields[2], fields[3]))
            ]

    for c in range(2):
        half = pool(residuals[c][:, 0:128], c, None, 0, 4, 8)
        for j in range(8):
            stacked[j * 16 + c * 8 : j * 16 + c * 8 + 8, :] = half
    pick = jnp.where(own_column & (lane8 % 8 == 0), 0.25, 0.0)
    column_source[1, a] = one_row(exact_dot(pick, stacked[...], True))
    start_columns(column_source, source_send, source_recv)
    hear("gy")
    tell("gy")

    def assembled(slots, fills):
        parts = ([], [])
        for col in range(3):
            for t in range(2):
                block = jnp.zeros((8, 128), F32)
                for j in range(gx_count):
                    row = jnp.broadcast_to(slots[col, j], (8, 128))
                    moved = pltpu.roll(
                        row, 8 - t * 8, axis=1, stride=16, stride_axis=0
                    )
                    block = jnp.where(lane8 // 8 == j, moved, block)
                if gx_count < 16:
                    block = jnp.where(lane8 // 8 < gx_count, block, fills[t])
                if col != 1:
                    limit = jnp.where(has_left if col == 0 else has_right, 128, 0)
                    block = jnp.where(lane8 < limit, block, fills[t])
                parts[t].append(block)
        return [
            jnp.concatenate([*parts[t], jnp.full((8, 128), fills[t], F32)], axis=0)
            for t in range(2)
        ]

    def closed_rows(shape, pitch, columns_too):
        first_col = iota(shape, 0) == (0 if columns_too else -1)
        return first_col, iota(shape, 1) < pitch

    finish_columns(column_coef, coef_send, coef_recv)
    reaction, viscous = assembled(column_coef, (1.0, 0.0))
    mid_faces = []
    for level in (4, 5):
        pitch = 2 ** (level - 4)
        closed = closed_rows(viscous.shape, pitch, False)
        mid_faces.append(coefficients(viscous, reaction, level, pitch, closed))
        reaction, viscous = pool(reaction, 2, pitch), pool(viscous, 3, pitch)

    def level6_row(x, y):
        x, y = jnp.where(lane8 % 4 == 0, x, 0.0), jnp.where(lane8 % 4 == 0, y, 0.0)
        both = x + roll_lanes(y, 1)
        return both[2:3] + roll_lanes(both[3:4], 2)

    def hops(k):
        x, y = k // 8, k % 8
        return min(x, 4 - x) + min(y, 8 - y)

    gy_order = sorted(range(1, gy_count), key=lambda k: -hops(k))

    def start_row(slots, sem):
        for k in gy_order:
            remote(slots.at[b], slots.at[b], gather_send.at[sem], gather_recv.at[sem], 0, k).start()

    def finish_row(slots, sem):
        rest = slots.at[pl.ds(0, gy_count - 1)]
        remote(rest, rest, gather_send.at[sem], gather_recv.at[sem], 0, 1).wait()

    hear("gy")
    assert reach["gy"] >= gy_count // 2
    gy_coef[b, 0:1, :] = level6_row(reaction, reaction)
    gy_coef[b, 1:2, :] = level6_row(viscous, viscous)
    start_row(gy_coef, 0)

    finish_columns(column_source, source_send, source_recv)
    source4 = assembled(column_source, (0.0, 0.0))
    source5 = [
        pool(residual_of(x, x * mid_faces[0][4], mid_faces[0], 1), c, 1)
        for c, x in enumerate(source4)
    ]
    source6 = [
        pool(residual_of(x, x * mid_faces[1][4], mid_faces[1], 2), c, 2)
        for c, x in enumerate(source5)
    ]
    gy_source[b] = level6_row(*source6)
    start_row(gy_source, 1)

    def spread_rows(x, i=0):
        n = x.shape[0]
        parts = []
        for t in range(x.shape[1] // 128):
            piece = x[:, t * 128 : t * 128 + 128]
            spread[i, t, pl.ds(0, n, stride=2), :] = piece
            spread[i, t, pl.ds(1, n, stride=2), :] = piece
            start = PAD if 2 * n > ROWS else 0
            parts.append(spread[i, t, start : 2 * n - start, :])
        return parts[0] if len(parts) == 1 else jnp.concatenate(parts, axis=1)

    def widened(x, pitch, i=0):
        odd = (iota((1, x.shape[1]), 1) & pitch) != 0
        return spread_rows(jnp.where(odd, roll_lanes(x, pitch), x), i)

    cols6 = 64

    def whole(read, i):
        for j in range(gy_count):
            coarse[i, 64 + j : 65 + j, :] = read(j)
        rows = coarse[i, 64:96, :]
        coarse[i, pl.ds(0, 32, stride=2), :] = rows
        coarse[i, pl.ds(1, 32, stride=2), :] = roll_lanes(rows, -2)
        return coarse[i, 0:cols6, :]

    if gy_count * 2 < cols6:
        coarse[...] = jnp.zeros_like(coarse)

    finish_row(gy_coef, 0)
    reaction = whole(lambda j: gy_coef[j, 0:1, :], 0)
    viscous = whole(lambda j: gy_coef[j, 1:2, :], 1)
    if gx_count * 2 < 32 or gy_count * 2 < cols6:
        reaction = jnp.where(reaction == 0.0, 1.0, reaction)
    coarse_faces = []
    for level in range(6, 9):
        pitch = 2 ** (level - 4)
        closed = closed_rows(viscous.shape, pitch, True)
        coarse_faces.append(coefficients(viscous, reaction, level, pitch, closed))
        if level < 8:
            reaction, viscous = pool(reaction, 2, pitch), pool(viscous, 3, pitch)
    up, down, left, right, weight8 = coarse_faces[2]
    scaled8 = (weight8 * up, weight8 * down, weight8 * left, weight8 * right)

    take_cols = jnp.where(
        iota((16, cols6), 1) == 2 * b - 2 + iota((16, cols6), 0) // 2, 1.0, 0.0
    )
    rows_back = jnp.where(
        iota((24, 128), 1) == 8 * a + (iota((24, 128), 0) + 4) // 2 - 4, 1.0, 0.0
    )
    fine = iota((32, 256), 1)
    fine = jnp.where(fine < 192, fine + 256, fine)
    cols_back = jnp.where(iota((32, 256), 0) == fine // 16 - 8, 1.0, 0.0)

    finish_row(gy_source, 1)
    source = whole(lambda j: gy_source[j], 2)
    coarse_sources = []
    for level in (6, 7):
        pitch = 2 ** (level - 4)
        faces = coarse_faces[level - 6]
        coarse_sources.append(source)
        source = pool(residual_of(source, source * faces[4], faces, pitch), 0, pitch)
    start = weight8 * source
    now = start
    for _ in range(7):
        now = (KEEP * now + start) + inflow(now, scaled8, 16)
    for level in (7, 6):
        pitch = 2 ** (level - 4)
        faces = coarse_faces[level - 6]
        source = coarse_sources[level - 6]
        now = swept(source, source * faces[4] + widened(now, pitch), faces, pitch)

    near = exact_dot(take_cols, now)
    lane16 = iota((16, 128), 1)
    current = []
    for c in range(2):
        mine = jnp.where(lane16 % 4 == c, near, 0.0)
        mine = roll_lanes(mine, -c) if c else mine
        correction = mine + roll_lanes(mine, 2)
        x = source5[c]
        result = swept(x, x * mid_faces[1][4] + correction, mid_faces[1], 2)
        x = source4[c]
        result = swept(x, x * mid_faces[0][4] + widened(result, 1, c), mid_faces[0], 1)
        current.append(exact_dot(exact_dot(rows_back, result, True), cols_back))

    for level in (3, 2, 1, 0):
        pitch = 2**level
        keep = stores[level]
        faces = [keep[j] for j in range(5)]
        for c in range(2):
            source = keep[5 + c]
            correction = current[c] if level == 3 else widened(current[c], pitch, c)
            result = swept(source, source * faces[4] + correction, faces, pitch)
            if level == 0:
                out_ref[c] = result[HALO : HALO + TILE, 0:128]
            else:
                current[c] = result


def solution(mesh):
    gx_count, gy_count = mesh.shape["gx"], mesh.shape["gy"]

    def per_device(right_side, shift_coef, viscosity, wet_tiles):
        hbm = pl.BlockSpec(memory_space=pltpu.HBM)
        dma = pltpu.SemaphoreType.DMA
        inner = (ROWS + 2 * PAD) // 2
        return pl.pallas_call(
            functools.partial(kernel, gx_count, gy_count),
            out_shape=pltpu.VMEM((2, TILE, TILE), F32),
            in_specs=[hbm, hbm, hbm, hbm],
            out_specs=pl.BlockSpec(memory_space=pltpu.VMEM),
            scratch_shapes=[
                pltpu.VMEM((4, TILE, TILE), F32),
                pltpu.SMEM((1, 1), jnp.int32),
                pltpu.VMEM((2, TILE, 128), F32),
                pltpu.VMEM((2, 4, HALO, 128), F32),
                pltpu.VMEM((2, TILE, 128), F32),
                pltpu.VMEM((4, HALO, 128), F32),
                pltpu.VMEM((3, gx_count, 1, 128), F32),
                pltpu.VMEM((3, gx_count, 1, 128), F32),
                pltpu.VMEM((gy_count, 2, 128), F32),
                pltpu.VMEM((gy_count, 1, 128), F32),
                pltpu.VMEM((4, ROWS, 256), F32),
                pltpu.VMEM((4, 2, ROWS + 2 * PAD, 128), F32),
                pltpu.VMEM((7, ROWS, 256), F32),
                pltpu.VMEM((7, inner, 256), F32),
                pltpu.VMEM((7, inner // 2, 256), F32),
                pltpu.VMEM((7, inner // 4, 256), F32),
                pltpu.VMEM((128, 128), F32),
                pltpu.VMEM((2, 2, ROWS + 2 * PAD, 128), F32),
                pltpu.VMEM((3, 96, 128), F32),
                dma((4,)),
                dma((8,)),
                dma((8,)),
                dma((3,)),
                dma((3,)),
                dma((3,)),
                dma((3,)),
                dma((2,)),
                dma((2,)),
                pltpu.SemaphoreType.REGULAR((16,)),
            ],
            compiler_params=pltpu.CompilerParams(collective_id=0, has_side_effects=True),
            name="vcycle",
        )(right_side, shift_coef, viscosity, wet_tiles)

    placed = (P(None, "gx", "gy"), P("gx", "gy"), P("gx", "gy"), P("gx", "gy"))
    return jax.shard_map(
        per_device, mesh=mesh, in_specs=placed, out_specs=P(None, "gx", "gy"), check_vma=False
    )
```

```python
import functools

import jax
import jax.numpy as jnp
from jax import lax
from jax.experimental import pallas as pl
from jax.experimental.pallas import tpu as pltpu
from jax.sharding import PartitionSpec as P

TILE = 128
OMEGA = 0.8
KEEP = 1.0 - OMEGA
HALO = 24
ROWS = TILE + 2 * HALO
PAD = 8
F32 = jnp.float32
MESH = pl.DeviceIdType.MESH
DIRECTIONS = ((-1, 0), (1, 0), (0, -1), (0, 1), (-1, -1), (-1, 1), (1, -1), (1, 1))


def iota(shape, dim):
    return lax.broadcasted_iota(jnp.int32, shape, dim)


def roll_rows(x, k):
    return pltpu.roll(x, k % x.shape[0], axis=0)


def roll_lanes(x, k):
    return pltpu.roll(x, k % x.shape[1], axis=1)


def exact_dot(a, b, transposed=False):
    dims = (((1,), (1,)), ((), ())) if transposed else (((1,), (0,)), ((), ()))
    return lax.dot_general(
        a, b, dims, precision=lax.Precision.HIGHEST, preferred_element_type=F32
    )


def picked(x, one_hot, left=False):
    total = None
    for _ in range(3):
        piece = x.astype(jnp.bfloat16)
        x = x - piece.astype(F32)
        if left:
            dims, pair = (((1,), (1,)), ((), ())), (one_hot, piece)
        else:
            dims, pair = (((1,), (0,)), ((), ())), (piece, one_hot)
        part = lax.dot_general(*pair, dims, preferred_element_type=F32)
        total = part if total is None else total + part
    return total


def coefficients(viscous, reaction, level, pitch, closed=None):
    spacing = 0.25**level
    up = jnp.minimum(viscous, roll_rows(viscous, 1)) * spacing
    left = jnp.minimum(viscous, roll_lanes(viscous, pitch)) * spacing
    if closed is not None:
        up = jnp.where(closed[0], 0.0, up)
        left = jnp.where(closed[1], 0.0, left)
    down = roll_rows(up, -1)
    right = roll_lanes(left, -pitch)
    weight = OMEGA / (reaction + ((up + down) + (left + right)))
    return up, down, left, right, weight


def inflow(iterate, faces, pitch):
    up, down, left, right = faces[:4]
    return (up * roll_rows(iterate, 1) + down * roll_rows(iterate, -1)) + (
        left * roll_lanes(iterate, pitch) + right * roll_lanes(iterate, -pitch)
    )


def residual_of(source, iterate, faces, pitch):
    return KEEP * source + inflow(iterate, faces, pitch)


def scaled(faces):
    return tuple(faces[4] * face for face in faces[:4])


def corrected(base, correction, faces, pitch):
    return (base + KEEP * correction) + inflow(correction, faces, pitch)


def swept(source, iterate, faces, pitch):
    return KEEP * iterate + faces[4] * (source + inflow(iterate, faces, pitch))


def kernel(
    gx_count,
    gy_count,
    rhs_hbm,
    shift_hbm,
    visc_hbm,
    wet_hbm,
    out_ref,
    own,
    wet_ref,
    strips,
    row_halo,
    col_halo,
    corner_halo,
    column_coef,
    column_source,
    gy_coef,
    gy_source,
    ext,
    pooled,
    level0,
    level1,
    level2,
    level3,
    stacked,
    spread,
    coarse,
    final,
    load_sem,
    halo_send,
    halo_recv,
    coef_send,
    coef_recv,
    source_send,
    source_recv,
    gather_send,
    gather_recv,
    known,
):
    a = lax.axis_index("gx")
    b = lax.axis_index("gy")
    has_up, has_down = a > 0, a < gx_count - 1
    has_left, has_right = b > 0, b < gy_count - 1
    has_row = {-1: has_up, 1: has_down}
    has_col = {-1: has_left, 1: has_right}

    def exists(da, db):
        if da == 0:
            return has_col[db]
        if db == 0:
            return has_row[da]
        return jnp.logical_and(has_row[da], has_col[db])

    barrier = pltpu.get_barrier_semaphore()

    def around(da, db):
        return (lax.rem(a + da + gx_count, gx_count), lax.rem(b + db + gy_count, gy_count))

    for da, db in DIRECTIONS[4:] + DIRECTIONS[:4]:
        pl.semaphore_signal(barrier, inc=1, device_id=around(da, db), device_id_type=MESH)

    loads = [
        pltpu.make_async_copy(wet_hbm, wet_ref, load_sem.at[3]),
        pltpu.make_async_copy(visc_hbm, own.at[3], load_sem.at[2]),
        pltpu.make_async_copy(rhs_hbm, own.at[pl.ds(0, 2)], load_sem.at[0]),
        pltpu.make_async_copy(shift_hbm, own.at[2], load_sem.at[1]),
    ]
    for load in loads:
        load.start()

    reach = {"gx": 1, "gy": 1}

    def tell(axis):
        r, count = reach[axis], gx_count if axis == "gx" else gy_count
        if r < count // 2:
            sem = known.at[(0 if axis == "gx" else 8) + r.bit_length()]
            for step in (r, -r):
                peer = around(step, 0) if axis == "gx" else around(0, step)
                pl.semaphore_signal(sem, inc=1, device_id=peer, device_id_type=MESH)

    def hear(axis):
        r, count = reach[axis], gx_count if axis == "gx" else gy_count
        if r < count // 2:
            sem = known.at[(0 if axis == "gx" else 8) + r.bit_length()]
            pl.semaphore_wait(sem, 2)
            reach[axis] = 2 * r

    for f in range(4):
        for t in range(2):
            edge = jnp.full((PAD, 128), 1.0 if f == 2 else 0.0, F32)
            pooled[f, t, 0:PAD, :] = edge
            pooled[f, t, PAD + ROWS :, :] = edge
    for load in loads:
        load.wait()

    wet = wet_ref[0, 0].astype(F32)
    for f in (0, 1, 3):
        own[f] = own[f] * wet

    slot = iota((TILE, 128), 1) // 32
    for side, first in ((0, 0), (1, TILE - HALO)):
        packed = roll_lanes(own[0], -first)
        for f in range(1, 4):
            packed = jnp.where(slot == f, roll_lanes(own[f], f * 32 - first), packed)
        strips[side] = packed

    pl.semaphore_wait(barrier, 8)

    def remote(src, dst, send_sem, recv_sem, da, db):
        return pltpu.make_async_remote_copy(
            src_ref=src,
            dst_ref=dst,
            send_sem=send_sem,
            recv_sem=recv_sem,
            device_id=around(da, db),
            device_id_type=MESH,
        )

    halo_copies = []
    for i, (da, db) in enumerate(DIRECTIONS):
        first = 0 if da < 0 else TILE - HALO
        if db == 0:
            src, dst = own.at[:, pl.ds(first, HALO)], row_halo.at[i]
        elif da == 0:
            src, dst = strips.at[0 if db < 0 else 1], col_halo.at[i - 2]
        else:
            src = strips.at[0 if db < 0 else 1, pl.ds(first, HALO)]
            dst = corner_halo.at[i - 4]
        copy = remote(src, dst, halo_send.at[i], halo_recv.at[i], da, db)
        halo_copies.append(copy)
    for i in (4, 5, 6, 7, 2, 3, 0, 1):
        pl.when(exists(*DIRECTIONS[i]))(halo_copies[i].start)
    tell("gx")
    tell("gy")

    gx_order = sorted(range(1, gx_count), key=lambda k: -min(k, gx_count - k))

    def start_columns(slots, sends, recvs):
        half = gx_count // 2
        for part in (slice(0, half), slice(half, gx_count)):
            for db in (-1, 1, 0):
                ks = [*gx_order, 0][part] if db else gx_order[part]

                def start(ks=ks, db=db):
                    for k in ks:
                        remote(
                            slots.at[1, a],
                            slots.at[1 - db, a],
                            sends.at[db + 1],
                            recvs.at[1 - db],
                            k,
                            db,
                        ).start()

                if db == 0:
                    start()
                else:
                    pl.when(has_col[db])(start)

    def finish_columns(slots, sends, recvs):
        for db in (-1, 1, 0):
            count = gx_count - 1 if db == 0 else gx_count
            every = remote(
                slots.at[1 - db, pl.ds(0, count)],
                slots.at[1 - db, pl.ds(0, count)],
                sends.at[db + 1],
                recvs.at[1 + db],
                1,
                0,
            )
            if db == 0:
                every.wait()
            else:
                pl.when(has_col[db])(every.wait)

    lane8 = iota((8, 128), 1)
    own_column = lane8 // 16 == iota((8, 128), 0)
    average = jnp.where(own_column, 0.0625, 0.0)
    to_lane = iota((128, 128), 1)
    from_row = iota((128, 128), 0)
    total = jnp.zeros((8, 128), F32)
    for f in range(2):
        to_row = jnp.where(
            (from_row // 16 == to_lane % 8) & (to_lane // 8 % 2 == f), 0.0625, 0.0
        )
        total = total + exact_dot(exact_dot(average, own[2 + f], True), to_row)

    def one_row(x):
        mine = jnp.where(lane8 // 16 == 7 - iota((8, 128), 0), x, 0.0)
        turned = pltpu.roll(mine, lax.rem(8 * a + 8, 128), axis=1)
        return jnp.sum(turned, axis=0, keepdims=True)

    column_coef[1, a] = one_row(total)
    hear("gx")
    tell("gx")
    hear("gy")
    tell("gy")

    for f in range(4):
        ext[f, HALO : HALO + TILE, 0:128] = own[f]
    hear("gx")
    tell("gx")
    for i, (da, db) in enumerate(DIRECTIONS):
        pl.when(exists(da, db))(halo_copies[i].wait_send)
        pl.when(exists(-da, -db))(halo_copies[i].wait_recv)

    lane = iota((1, 128), 1)
    all_up = lane < jnp.where(has_up, 128, 0)
    all_down = lane < jnp.where(has_down, 128, 0)
    beside = (lane < jnp.where(has_right, HALO, 0)) | (
        lane >= jnp.where(has_left, TILE - HALO, 128)
    )
    for f in range(4):
        fill = 1.0 if f == 2 else 0.0
        ext[f, 0:HALO, 0:128] = jnp.where(all_up, row_halo[1, f], fill)
        ext[f, HALO + TILE :, 0:128] = jnp.where(all_down, row_halo[0, f], fill)

        def side(right, left, valid):
            r = roll_lanes(right, -f * 32)
            l = roll_lanes(left, TILE - HALO - f * 32)
            return jnp.where(valid, jnp.where(lane < 64, r, l), fill)

        ext[f, HALO : HALO + TILE, 128:256] = side(col_halo[0], col_halo[1], beside)
        ext[f, 0:HALO, 128:256] = side(corner_halo[2], corner_halo[3], beside & all_up)
        ext[f, HALO + TILE :, 128:256] = side(corner_halo[0], corner_halo[1], beside & all_down)

    def pool(x, i, pitch, first=0, start=0, rows=None):
        n = x.shape[0]
        width = x.shape[1]
        rows = n // 2 if rows is None else rows
        parts = []
        for t in range(width // 128):
            pooled[i, t, first : first + n, :] = x[:, t * 128 : t * 128 + 128]
            parts.append(
                pooled[i, t, pl.ds(start, rows, stride=2), :]
                + pooled[i, t, pl.ds(start + 1, rows, stride=2), :]
            )
        y = parts[0] if len(parts) == 1 else jnp.concatenate(parts, axis=1)
        return y if pitch is None else (y + roll_lanes(y, -pitch)) * 0.25

    turned_row = lax.rem(iota((128, 128), 0) + (256 - 8 - 8 * a), 128)
    pairs = (to_lane // 16 == 7 - turned_row // 16) & (to_lane % 8 == 0)
    quarter = jnp.full((8, 128), 0.25, jnp.bfloat16)

    fields = [ext[f] for f in range(4)]
    stores = (level0, level1, level2, level3)
    for level in range(4):
        pitch = 2**level
        keep = stores[level]
        faces = coefficients(fields[3], fields[2], level, pitch)
        for j in range(5):
            keep[j] = faces[j]
        residuals = []
        for c in range(2):
            iterate = fields[c] * faces[4]
            keep[5 + c] = fields[c]
            residuals.append(residual_of(fields[c], iterate, faces, pitch))
        if level == 0:
            hear("gy")
            tell("gy")
        if level == 1:
            hear("gx")
            assert reach["gx"] >= gx_count // 2
            start_columns(column_coef, coef_send, coef_recv)
        if level < 3:
            shape = (PAD, 0, (ROWS + 2 * PAD) // 2) if level == 0 else (0, 0, None)
            fields = [
                pool(x, i, pitch, *shape)
                for i, x in enumerate((*residuals, fields[2], fields[3]))
            ]

    for c in range(2):
        half = pool(residuals[c][:, 0:128], c, None, 0, 4, 8)
        for j in range(8):
            place = lax.rem(8 * a + (j * 16 + c * 8 + 8), 128)
            stacked[pl.ds(pl.multiple_of(place, 8), 8), :] = half
    paired = jnp.where(pairs, stacked[...], 0.0)
    column_source[1, a] = picked(paired, quarter, True)[0:1]
    start_columns(column_source, source_send, source_recv)

    inside = slice(HALO, HALO + TILE)
    for level in range(4):
        pitch = 2**level
        keep = stores[level]
        faces = [keep[j] for j in range(5)]
        for c in range(2):
            base = swept(keep[5 + c], keep[5 + c] * faces[4], faces, pitch)
            if level == 0:
                final[4 + c] = base[inside, 0:128]
            else:
                keep[5 + c] = base
        for j, face in enumerate(scaled(faces)):
            if level == 0:
                final[j] = face[inside, 0:128]
            else:
                keep[j] = face
    hear("gy")
    tell("gy")

    def assembled(slots, fills):
        parts = ([], [])
        for col in range(3):
            for t in range(2):
                block = jnp.zeros((8, 128), F32)
                for j in range(gx_count):
                    row = jnp.broadcast_to(slots[col, j], (8, 128))
                    moved = pltpu.roll(
                        row, 8 - t * 8, axis=1, stride=16, stride_axis=0
                    )
                    block = jnp.where(lane8 // 8 == j, moved, block)
                if gx_count < 16:
                    block = jnp.where(lane8 // 8 < gx_count, block, fills[t])
                if col != 1:
                    limit = jnp.where(has_left if col == 0 else has_right, 128, 0)
                    block = jnp.where(lane8 < limit, block, fills[t])
                parts[t].append(block)
        return [
            jnp.concatenate([*parts[t], jnp.full((8, 128), fills[t], F32)], axis=0)
            for t in range(2)
        ]

    def closed_rows(shape, pitch, columns_too):
        first_col = iota(shape, 0) == (0 if columns_too else -1)
        return first_col, iota(shape, 1) < pitch

    finish_columns(column_coef, coef_send, coef_recv)
    reaction, viscous = assembled(column_coef, (1.0, 0.0))
    mid_faces = []
    for level in (4, 5):
        pitch = 2 ** (level - 4)
        closed = closed_rows(viscous.shape, pitch, False)
        mid_faces.append(coefficients(viscous, reaction, level, pitch, closed))
        reaction, viscous = pool(reaction, 2, pitch), pool(viscous, 3, pitch)

    def level6_row(x, y):
        x, y = jnp.where(lane8 % 4 == 0, x, 0.0), jnp.where(lane8 % 4 == 0, y, 0.0)
        first = x + roll_lanes(y, 1)
        second = roll_lanes(x, 2) + roll_lanes(y, 3)
        return first[2:3] + second[3:4]

    def hops(k):
        x, y = k // 8, k % 8
        return min(x, 4 - x) + min(y, 8 - y)

    gy_order = sorted(range(1, gy_count), key=lambda k: -hops(k))

    def start_row(slots, sem):
        for k in gy_order:
            remote(slots.at[b], slots.at[b], gather_send.at[sem], gather_recv.at[sem], 0, k).start()

    def finish_row(slots, sem):
        rest = slots.at[pl.ds(0, gy_count - 1)]
        remote(rest, rest, gather_send.at[sem], gather_recv.at[sem], 0, 1).wait()

    hear("gy")
    assert reach["gy"] >= gy_count // 2
    gy_coef[b, 0:1, :] = level6_row(reaction, reaction)
    gy_coef[b, 1:2, :] = level6_row(viscous, viscous)
    start_row(gy_coef, 0)

    finish_columns(column_source, source_send, source_recv)
    source4 = assembled(column_source, (0.0, 0.0))
    source5 = [
        pool(residual_of(x, x * mid_faces[0][4], mid_faces[0], 1), c, 1)
        for c, x in enumerate(source4)
    ]
    source6 = [
        pool(residual_of(x, x * mid_faces[1][4], mid_faces[1], 2), c, 2)
        for c, x in enumerate(source5)
    ]
    gy_source[b] = level6_row(*source6)
    start_row(gy_source, 1)
    base4 = [swept(x, x * mid_faces[0][4], mid_faces[0], 1) for x in source4]
    base5 = [swept(x, x * mid_faces[1][4], mid_faces[1], 2) for x in source5]
    scaled4, scaled5 = scaled(mid_faces[0]), scaled(mid_faces[1])

    def spread_rows(x, i=0):
        n = x.shape[0]
        parts = []
        for t in range(x.shape[1] // 128):
            piece = x[:, t * 128 : t * 128 + 128]
            spread[i, t, pl.ds(0, n, stride=2), :] = piece
            spread[i, t, pl.ds(1, n, stride=2), :] = piece
            start = PAD if 2 * n > ROWS else 0
            parts.append(spread[i, t, start : 2 * n - start, :])
        return parts[0] if len(parts) == 1 else jnp.concatenate(parts, axis=1)

    def widened(x, pitch, i=0):
        odd = (iota((1, x.shape[1]), 1) & pitch) != 0
        return spread_rows(jnp.where(odd, roll_lanes(x, pitch), x), i)

    cols6 = 64

    def whole(rows, i):
        coarse[i, pl.ds(0, gy_count, stride=2), :] = rows
        coarse[i, pl.ds(1, gy_count, stride=2), :] = roll_lanes(rows, -2)
        return coarse[i]

    if gy_count * 2 < cols6:
        coarse[...] = jnp.zeros_like(coarse)

    finish_row(gy_coef, 0)
    reaction = whole(gy_coef[:, 0, :], 0)
    viscous = whole(gy_coef[:, 1, :], 1)
    if gx_count * 2 < 32 or gy_count * 2 < cols6:
        reaction = jnp.where(reaction == 0.0, 1.0, reaction)
    coarse_faces = []
    for level in range(6, 9):
        pitch = 2 ** (level - 4)
        closed = closed_rows(viscous.shape, pitch, True)
        coarse_faces.append(coefficients(viscous, reaction, level, pitch, closed))
        if level < 8:
            reaction, viscous = pool(reaction, 2, pitch), pool(viscous, 3, pitch)
    scaled8, weight8 = scaled(coarse_faces[2]), coarse_faces[2][4]
    coarse_scaled = [scaled(faces) for faces in coarse_faces[:2]]

    rows_back = iota((24, 128), 1) == 8 * a + (iota((24, 128), 0) + 4) // 2 - 4
    rows_back = jnp.where(rows_back, 1.0, 0.0).astype(jnp.bfloat16)
    fine = iota((32, 256), 1)
    fine = jnp.where(fine < 192, fine + 256, fine)
    cols_back = iota((32, 256), 0) == fine // 16 - 8
    cols_back = jnp.where(cols_back, 1.0, 0.0).astype(jnp.bfloat16)

    finish_row(gy_source, 1)
    source = whole(gy_source[:, 0, :], 2)
    bases = []
    for level in (6, 7):
        pitch = 2 ** (level - 4)
        faces = coarse_faces[level - 6]
        iterate = source * faces[4]
        around_it = inflow(iterate, faces, pitch)
        bases.append(KEEP * iterate + faces[4] * (source + around_it))
        source = pool(KEEP * source + around_it, 0, pitch)
    start = weight8 * source
    now = start
    for _ in range(7):
        now = corrected(start, now, scaled8, 16)
    for level in (7, 6):
        pitch = 2 ** (level - 4)
        now = corrected(bases[level - 6], widened(now, pitch), coarse_scaled[level - 6], pitch)

    near = spread_rows(pltpu.roll(now, lax.rem(cols6 + 2 - 2 * b, cols6), axis=0)[0:8])
    lane16 = iota((16, 128), 1)
    current = []
    for c in range(2):
        mine = jnp.where(lane16 % 4 == c, near, 0.0)
        mine = roll_lanes(mine, -c) if c else mine
        result = corrected(base5[c], mine + roll_lanes(mine, 2), scaled5, 2)
        result = corrected(base4[c], widened(result, 1, c), scaled4, 1)
        current.append(picked(picked(result, rows_back, True), cols_back))

    for level in (3, 2, 1):
        pitch = 2**level
        keep = stores[level]
        faces = [keep[j] for j in range(4)]
        for c in range(2):
            correction = current[c] if level == 3 else widened(current[c], pitch, c)
            current[c] = corrected(keep[5 + c], correction, faces, pitch)

    for c in range(2):
        correction = widened(current[c], 1, c)
        here, beyond = correction[:, 0:128], correction[inside, 128:256]
        own_rows = here[inside]
        before = jnp.where(lane == 0, roll_lanes(beyond, 1), roll_lanes(own_rows, 1))
        after = jnp.where(lane == 127, roll_lanes(beyond, -1), roll_lanes(own_rows, -1))
        rows = (final[0] * roll_rows(here, 1)[inside] + final[1] * roll_rows(here, -1)[inside])
        out_ref[c] = (final[4 + c] + KEEP * own_rows) + (rows + (final[2] * before + final[3] * after))


def solution(mesh):
    gx_count, gy_count = mesh.shape["gx"], mesh.shape["gy"]

    def per_device(right_side, shift_coef, viscosity, wet_tiles):
        hbm = pl.BlockSpec(memory_space=pltpu.HBM)
        dma = pltpu.SemaphoreType.DMA
        inner = (ROWS + 2 * PAD) // 2
        return pl.pallas_call(
            functools.partial(kernel, gx_count, gy_count),
            out_shape=pltpu.VMEM((2, TILE, TILE), F32),
            in_specs=[hbm, hbm, hbm, hbm],
            out_specs=pl.BlockSpec(memory_space=pltpu.VMEM),
            scratch_shapes=[
                pltpu.VMEM((4, TILE, TILE), F32),
                pltpu.SMEM((1, 1), jnp.int32),
                pltpu.VMEM((2, TILE, 128), F32),
                pltpu.VMEM((2, 4, HALO, 128), F32),
                pltpu.VMEM((2, TILE, 128), F32),
                pltpu.VMEM((4, HALO, 128), F32),
                pltpu.VMEM((3, gx_count, 1, 128), F32),
                pltpu.VMEM((3, gx_count, 1, 128), F32),
                pltpu.VMEM((gy_count, 2, 128), F32),
                pltpu.VMEM((gy_count, 1, 128), F32),
                pltpu.VMEM((4, ROWS, 256), F32),
                pltpu.VMEM((4, 2, ROWS + 2 * PAD, 128), F32),
                pltpu.VMEM((7, ROWS, 256), F32),
                pltpu.VMEM((7, inner, 256), F32),
                pltpu.VMEM((7, inner // 2, 256), F32),
                pltpu.VMEM((7, inner // 4, 256), F32),
                pltpu.VMEM((128, 128), F32),
                pltpu.VMEM((2, 2, ROWS + 2 * PAD, 128), F32),
                pltpu.VMEM((3, 64, 128), F32),
                pltpu.VMEM((6, TILE, TILE), F32),
                dma((4,)),
                dma((8,)),
                dma((8,)),
                dma((3,)),
                dma((3,)),
                dma((3,)),
                dma((3,)),
                dma((2,)),
                dma((2,)),
                pltpu.SemaphoreType.REGULAR((16,)),
            ],
            compiler_params=pltpu.CompilerParams(collective_id=0, has_side_effects=True),
            name="vcycle",
        )(right_side, shift_coef, viscosity, wet_tiles)

    placed = (P(None, "gx", "gy"), P("gx", "gy"), P("gx", "gy"), P("gx", "gy"))
    return jax.shard_map(
        per_device, mesh=mesh, in_specs=placed, out_specs=P(None, "gx", "gy"), check_vma=False
    )
```
